256 devices in a mesh: sq: 8 (over z), ex: 32 (over x, y, core).
Axes of the slice: x: 4, y: 4, z: 8, core: 2. Of those that a mesh axis runs over, the one named last changes fastest.
Arguments:
- tokens: bfloat16 [16384, 2048], P(('sq', 'ex')), may hold values from -6 to 6
- venue_id: int32 [16384], P(('sq', 'ex')), may hold values from 0 to 15
- time_rank: int32 [16384], replicated, may hold values from 0 to 16383, each once
- routes: int32 [16384, 6], P(('sq', 'ex')), may hold values from 0 to 31, all different within a row; in each aligned block of 64 rows (0 to 63, 64 to 127, ...) at most 30 rows name the same one
- venue_table: bfloat16 [16, 2048], replicated, may hold values from -3 to 3
- attn_gain: float32 [2048], replicated, may hold values from 0.8 to 8
- w_qkv: bfloat16 [2048, 3, 1024], P(None, None, 'sq'), may hold values from -0.125 to 0.125
- w_out: bfloat16 [1024, 2048], P('sq'), may hold values from -0.5 to 0.5
- ffn_gain: float32 [2048], replicated, may hold values from 0.5 to 1.5
- router: bfloat16 [2048, 32], replicated, may hold values from -0.125 to 0.125
- expert_in: bfloat16 [32, 2, 2048, 768], P('ex'), may hold values from -0.125 to 0.125
- expert_out: bfloat16 [32, 768, 2048], P('ex'), may hold values from -0.21875 to 0.21875
Outputs:
- attended: bfloat16 [16384, 2048], P(('sq', 'ex'))
- layer_out: bfloat16 [16384, 2048], P(('sq', 'ex'))
The draws below stay inside these ranges and needn't reach their ends.
Inputs may be any that keep to these rules, and one draw needn't show every extreme that they name: `routes`: each token names 6 different experts; among the 64 rows of one device no expert is named by more than 30 rows, and in every draw some expert is named by exactly 30 rows of some device. `time_rank`: each of 0 to 16383 appears once.
All inputs are finite; a program needn't handle non-finite values.
Results may differ from the reference program's by a relative error of at most 0.019.
The reference program's roundings to bfloat16 on the way count: a program that leaves them out, or rounds other values in their place, can miss the bound.
Values may be sent and summed in bfloat16 or wider, within the bound.
No kernel may reach another device: no remote copies, remote signals or barrier semaphores. Data moves between devices by JAX's collectives and lax.ppermute only.
A program may use at most 128 MiB of HBM per device.

```python
import math
import jax
import jax.numpy as jnp
import numpy as np
from jax import lax

D = 2048
HEAD_DIM = 128
FF = 768
TOP = 6
VENUES = 16
TOK_DEV = 64
HEADS = 8
EXPERTS = 32
TOKENS = 16384
CAP = 30
N_SQ = 8
N_EX = 32


def draw_attn_gain(key, part):
    return jax.random.uniform(key, (D,), jnp.float32, 0.8, 2.0)


def with_ends(drawn, stream_key, least, largest):
    longest = drawn.shape.index(max(drawn.shape))
    spots = []
    for shift in (0, 1):
        where = [jax.random.randint(jax.random.fold_in(stream_key, axis), (), 0, length) for axis, length in enumerate(drawn.shape)]
        where[longest] = (where[longest] + shift) % drawn.shape[longest]
        spots.append(tuple(where))
    return drawn.at[spots[0]].set(least).at[spots[1]].set(largest)


def steps_of(rng, shape, cuts, smallest, high):
    def one(axis_at, shards_of):
        steps = jax.random.uniform(jax.random.fold_in(jax.random.fold_in(rng, 6), axis_at), (shards_of,), jnp.float32, smallest / len(cuts), high / len(cuts))
        return jnp.repeat(jnp.exp(steps), shape[axis_at] // shards_of).reshape((-1,) + (1,) * (len(shape) - axis_at - 1))

    loudness = one(*cuts[0])
    for cut in cuts[1:]:
        loudness = loudness * one(*cut)
    return loudness


def shared_out(stream_key, own, number, rows, amount, top, reach, skew):
    sequence = jax.random.permutation(stream_key, amount)
    heavy_load, ordinary = load_shares(amount, rows * top, reach, skew, True), load_shares(amount, rows * top, reach, skew, False)
    places = jnp.arange(amount)

    def named(sizes, offset_by):
        used = int((sizes > 0).sum())
        fixed = max(1, used // 4)
        moved = fixed + (places - fixed + offset_by * (used - fixed)) % max(1, amount - fixed)
        return jnp.zeros((amount,), jnp.int32).at[sequence[jnp.where(places < fixed, places, moved)]].set(jnp.asarray(sizes, jnp.int32))

    sizes = jnp.where(number % 4 == 0, named(heavy_load, number // 4), named(ordinary, number - number // 4 - 1))
    mixed = jax.random.permutation(jax.random.fold_in(own, 3), amount)
    source_of, receiver = mixed[0:amount // 2 * 2:2], mixed[1:amount // 2 * 2:2]
    room = jnp.minimum(sizes[source_of] - 1, reach - sizes[receiver]) // 2
    room = jnp.where((source_of == sequence[0]) | (receiver == sequence[0]) | (sizes[receiver] == 0), 0, jnp.maximum(room, 0))
    moved = jax.random.randint(jax.random.fold_in(own, 4), (amount // 2,), 0, 1 << 20) % (room + 1)
    sizes = sizes.at[source_of].add(-moved).at[receiver].add(moved)
    labels = jnp.searchsorted(jnp.cumsum(sizes), jnp.arange(rows * top), side="right").astype(jnp.int32)
    listing = labels.reshape(top, rows).T
    listing = listing[jax.random.permutation(jax.random.fold_in(own, 1), rows)]
    offset_by = jax.random.randint(jax.random.fold_in(own, 2), (rows, 1), 0, top)
    return jnp.take_along_axis(listing, (jnp.arange(top)[None, :] + offset_by) % top, axis=1)


def load_shares(number_of, total, reach, lean, full):
    loads = [(1 << 20) // math.isqrt(grade ** lean) + 1 for grade in range(1, number_of + 1)]
    largest = reach if full else min(reach, max(-(-total // number_of), total * loads[0] // sum(loads)))
    least = 1 if total - largest >= number_of - 1 else 0
    given, surplus = [largest] + [least] * (number_of - 1), total - largest - least * (number_of - 1)
    while surplus > 0:
        candidates = [i for i in range(1, number_of) if given[i] < largest] or [i for i in range(1, number_of) if given[i] < reach]
        whole, budget = sum([loads[i] for i in candidates]), surplus
        for i in candidates:
            more = min(reach - given[i], max(1, budget * loads[i] // whole), surplus)
            given[i] = given[i] + more
            surplus = surplus - more
    return np.array(given)


def bell_draw(own_key, dims, spread, reach, cuts=(), held_as=jnp.bfloat16):
    level = steps_of(own_key, dims, cuts, -0.22, 0.18) if cuts else 1.0
    entries = jax.random.normal(own_key, dims, jnp.float32) * spread * level
    return jnp.minimum(jnp.maximum(entries, -reach), reach).astype(held_as)


def setup_inputs(seed: int = 0) -> dict:
    seeds = jax.random.split(jax.random.key(seed), 13)
    tokens = bell_draw(seeds[0], (TOKENS, D), 1.0, 6.0, ((0, 256),))
    venue_id = with_ends(jax.random.randint(seeds[1], (TOKENS,), 0, VENUES), jax.random.fold_in(seeds[1], 1), 0, VENUES - 1).astype(jnp.int32)
    time_rank = jax.random.permutation(seeds[2], TOKENS).astype(jnp.int32)
    routes_keys = jax.random.split(jax.random.fold_in(seeds[3], 1), TOKENS // TOK_DEV)
    routes_turns = jax.random.permutation(jax.random.fold_in(seeds[3], 3), TOKENS // TOK_DEV)
    routes = jax.vmap(lambda own, number: shared_out(jax.random.fold_in(seeds[3], 2), own, number, TOK_DEV, EXPERTS, TOP, CAP, 2))(routes_keys, routes_turns).reshape((TOKENS, TOP))
    venue_table = bell_draw(seeds[4], (VENUES, D), 0.5, 3.0)
    attn_gain = draw_attn_gain(jax.random.fold_in(seeds[12], 71), 0)
    w_qkv = bell_draw(seeds[6], (D, 3, HEADS * HEAD_DIM), D ** -0.5, 0.125, ((2, 8),))
    w_out = bell_draw(seeds[7], (HEADS * HEAD_DIM, D), HEAD_DIM ** -0.5, 0.5, ((0, 8),))
    ffn_gain = jnp.clip(1.0 + 0.1 * jax.random.normal(seeds[8], (D,), jnp.float32), 0.5, 1.5)
    router = bell_draw(seeds[9], (D, EXPERTS), D ** -0.5, 0.125)
    expert_in = bell_draw(seeds[10], (EXPERTS, 2, D, FF), D ** -0.5, 0.125, ((0, 32),))
    expert_out = bell_draw(seeds[11], (EXPERTS, FF, D), FF ** -0.5, 0.21875, ((0, 32),))
    return dict(tokens=tokens, venue_id=venue_id, time_rank=time_rank, routes=routes, venue_table=venue_table, attn_gain=attn_gain, w_qkv=w_qkv, w_out=w_out, ffn_gain=ffn_gain, router=router, expert_in=expert_in, expert_out=expert_out)


epsilon = 1e-06
neg_large = -1e+30

def rms_norm(values, gain):
    mean_square = lax.optimization_barrier(jnp.mean(values * values, axis=-1, keepdims=True))
    return values * lax.rsqrt(mean_square + epsilon) * gain

def attend_head(queries, key_rows, value_rows, time_rank):
    block_size = math.gcd(TOKENS, 1024)
    inv_scale = 1.0 / math.sqrt(HEAD_DIM)

    def one_block(index):
        first_row = (index * block_size).astype(jnp.int32)
        query_block = lax.dynamic_slice_in_dim(queries, first_row, block_size, 0)
        query_rank = lax.dynamic_slice_in_dim(time_rank, first_row, block_size, 0)
        scores = jnp.dot(query_block, key_rows.T, preferred_element_type=jnp.float32) * inv_scale
        allowed = time_rank[None, :] <= query_rank[:, None]
        masked = jnp.where(allowed, scores, neg_large)
        row_best = lax.optimization_barrier(jnp.max(masked, axis=1, keepdims=True))
        probs = jnp.where(allowed, jnp.exp(masked - row_best), 0.0)
        row_total = lax.optimization_barrier(jnp.sum(probs, axis=1, keepdims=True))
        mixed = jnp.dot(probs.astype(jnp.bfloat16), value_rows, preferred_element_type=jnp.float32)
        return (mixed / row_total).astype(jnp.bfloat16)
    blocks = lax.map(one_block, jnp.arange(TOKENS // block_size, dtype=jnp.int32))
    return blocks.reshape(TOKENS, HEAD_DIM)

def reference(tokens, venue_id, time_rank, routes, venue_table, attn_gain, w_qkv, w_out, ffn_gain, router, expert_in, expert_out):
    venue_hot = (venue_id[:, None] == jnp.arange(VENUES, dtype=jnp.int32)[None, :]).astype(jnp.bfloat16)
    base_rows = tokens.astype(jnp.float32) + jnp.dot(venue_hot, venue_table, preferred_element_type=jnp.float32)
    normed = rms_norm(base_rows, attn_gain).astype(jnp.bfloat16)
    projected = jnp.dot(normed, w_qkv.reshape(D, 3 * HEADS * HEAD_DIM), preferred_element_type=jnp.float32).astype(jnp.bfloat16)
    projected = projected.reshape(TOKENS, 3, HEADS, HEAD_DIM).transpose(1, 2, 0, 3)

    def per_head(items):
        return attend_head(items[0], items[1], items[2], time_rank)
    head_out = lax.map(per_head, (projected[0], projected[1], projected[2]))
    w_heads = w_out.reshape(HEADS, HEAD_DIM, D)

    def add_head(carry, items):
        partial_out = jnp.dot(items[0], items[1], preferred_element_type=jnp.float32).astype(jnp.bfloat16)
        return (carry + partial_out.astype(jnp.float32), None)
    attn_sum, unused = lax.scan(add_head, jnp.zeros((TOKENS, D), jnp.float32), (head_out, w_heads))
    hidden_state = base_rows + attn_sum
    normed_ffn = rms_norm(hidden_state, ffn_gain).astype(jnp.bfloat16)
    logits = jnp.dot(normed_ffn, router, preferred_element_type=jnp.float32)
    chosen = jnp.take_along_axis(logits, routes, axis=1)
    raw_gate = jax.nn.sigmoid(chosen)
    gate_weights = raw_gate / lax.optimization_barrier(jnp.sum(raw_gate, axis=1, keepdims=True))
    flat_routes = routes.reshape(-1)
    flat_gates = gate_weights.reshape(-1)
    sorted_pairs = jnp.argsort(flat_routes, stable=True).astype(jnp.int32)
    expert_ids = jnp.arange(EXPERTS, dtype=jnp.int32)
    counts = lax.optimization_barrier(jnp.sum((flat_routes[:, None] == expert_ids[None, :]).astype(jnp.int32), axis=0))
    starts = (jnp.cumsum(counts) - counts).astype(jnp.int32)
    max_rows = N_SQ * N_EX * CAP
    padded = jnp.concatenate([sorted_pairs, jnp.zeros((max_rows,), jnp.int32)])

    def add_expert(expert, moe_sum):
        picked = lax.dynamic_slice_in_dim(padded, starts[expert], max_rows, 0)
        live_rows = jnp.arange(max_rows, dtype=jnp.int32) < counts[expert]
        token_index = (picked // TOP).astype(jnp.int32)
        rows_in = normed_ffn[token_index]
        gate_part = jnp.dot(rows_in, expert_in[expert, 0], preferred_element_type=jnp.float32)
        up_part = jnp.dot(rows_in, expert_in[expert, 1], preferred_element_type=jnp.float32)
        hidden = (jax.nn.silu(gate_part) * up_part).astype(jnp.bfloat16)
        produced = jnp.dot(hidden, expert_out[expert], preferred_element_type=jnp.float32).astype(jnp.bfloat16)
        row_scale = jnp.where(live_rows, flat_gates[picked], 0.0)
        return moe_sum.at[token_index].add(row_scale[:, None] * produced.astype(jnp.float32))
    moe_sum = lax.fori_loop(0, EXPERTS, add_expert, jnp.zeros((TOKENS, D), jnp.float32))
    attended = attn_sum.astype(jnp.bfloat16)
    layer_out = (hidden_state + moe_sum).astype(jnp.bfloat16)
    return (attended, layer_out)
```

```python
import functools
import math

import jax
import jax.numpy as jnp
from jax import lax
from jax.experimental import pallas as pl
from jax.experimental.pallas import tpu as pltpu
from jax.sharding import PartitionSpec as P

epsilon = 1e-06
neg_large = -1e30


def rms_norm(values, gain):
    mean_square = jnp.mean(values * values, axis=-1, keepdims=True)
    return values * lax.rsqrt(mean_square + epsilon) * gain


def flash_kernel(key_step, scale, query_ref, keyval_ref, query_rank_ref, key_rank_ref, state_ref, out_ref):
    head_dim = query_ref.shape[1]
    queries = query_ref[...]
    query_count = queries.shape[0]
    query_rank = query_rank_ref[...]
    out_ref[...] = state_ref[...]

    def step(j, carry):
        row_best, row_total = carry
        start = pl.multiple_of(j * key_step, key_step)
        keys = keyval_ref[pl.ds(start, key_step), :head_dim]
        values = keyval_ref[pl.ds(start, key_step), head_dim:]
        scores = lax.dot_general(
            keys, queries, (((1,), (1,)), ((), ())), preferred_element_type=jnp.float32
        )
        key_rank = key_rank_ref[pl.ds(start, key_step), :]
        key_rank = jnp.concatenate([key_rank] * (query_count // 128), axis=1)
        scores = jnp.where(key_rank <= query_rank, scores, neg_large)
        new_best = jnp.maximum(row_best, jnp.max(scores, axis=0, keepdims=True))
        probs = jnp.exp2((scores - new_best) * scale)
        factor = jnp.exp2((row_best - new_best) * scale)
        row_total = row_total * factor + jnp.sum(probs, axis=0, keepdims=True)
        update = lax.dot_general(
            values,
            probs.astype(jnp.bfloat16),
            (((0,), (0,)), ((), ())),
            preferred_element_type=jnp.float32,
        )
        out_ref[:head_dim] = out_ref[:head_dim] * factor + update
        return new_best, row_total

    carry = (state_ref[head_dim : head_dim + 1], state_ref[head_dim + 4 : head_dim + 5])
    best, total = lax.fori_loop(0, keyval_ref.shape[0] // key_step, step, carry)
    out_ref[head_dim:] = jnp.concatenate(
        [jnp.broadcast_to(best, (4, query_count)), jnp.broadcast_to(total, (4, query_count))],
        axis=0,
    )


def flash_part(queries, keyval, query_rank, key_rank, state):
    head_dim = queries.shape[1]
    scale = math.log2(math.e) / math.sqrt(head_dim)
    wide_rank = jnp.broadcast_to(key_rank[:, None], (key_rank.shape[0], 128))
    return pl.pallas_call(
        functools.partial(flash_kernel, 1024, scale),
        out_shape=jax.ShapeDtypeStruct(state.shape, jnp.float32),
        name="flash_part",
        compiler_params=pltpu.CompilerParams(vmem_limit_bytes=48 << 20),
    )(queries, keyval, query_rank[None, :], wide_rank, state)


side = 4
cores = 2
hops = (0, 1, 3, 2)


def ex_id(x, y, c):
    return (x % side) * side * cores + (y % side) * cores + c


def plane_shift(array, amount, first):
    pairs = []
    for x in range(side):
        for y in range(side):
            for c in range(cores):
                if (c == 0) == first:
                    target = ex_id(x + amount, y, c)
                else:
                    target = ex_id(x, y + amount, c)
                pairs.append((ex_id(x, y, c), target))
    return lax.ppermute(array, "ex", pairs)


def plane_gather(array):
    line = jnp.concatenate(
        [array] + [plane_shift(array, s, True) for s in hops[1:]], axis=0
    )
    return jnp.concatenate([line] + [plane_shift(line, s, False) for s in hops[1:]], axis=0)


def plane_sources(ex_index, core):
    x = ex_index // (side * cores)
    y = ex_index // cores % side
    second = jnp.repeat(jnp.array(hops, jnp.int32), side)
    first = jnp.tile(jnp.array(hops, jnp.int32), side)
    shift_x = jnp.where(core == 0, first, second)
    shift_y = jnp.where(core == 0, second, first)
    return (x - shift_x) % side * side * cores + (y - shift_y) % side * cores + core


def core_swap(array):
    return lax.ppermute(array, "ex", [(i, i ^ 1) for i in range(side * side * cores)])


def ring_shift(array, amount):
    count = lax.axis_size("sq")
    return lax.ppermute(array, "sq", [(i, (i + amount) % count) for i in range(count)])


def ring_gather(array):
    half = array.shape[0] // 2
    p1 = ring_shift(array, 1)
    m1 = ring_shift(array, -1)
    p2 = ring_shift(array, 2)
    m2 = ring_shift(array, -2)
    p3 = ring_shift(p2, 1)
    m3 = ring_shift(m2, -1)
    p4 = ring_shift(p2[:half], 2)
    m4 = ring_shift(m2[half:], -2)
    return jnp.concatenate([p3, p2, p1, array, m1, m2, m3, p4, m4], axis=0)


def body(
    tokens,
    venue_id,
    time_rank,
    routes,
    venue_table,
    attn_gain,
    w_qkv,
    w_out,
    ffn_gain,
    router,
    expert_in,
    expert_out,
):
    tok_rows, model_width = tokens.shape
    head_dim = w_out.shape[0]
    sq_count = lax.axis_size("sq")
    ex_count = lax.axis_size("ex")
    ex_index = lax.axis_index("ex")
    venue_hot = (
        venue_id[:, None] == jnp.arange(venue_table.shape[0], dtype=jnp.int32)[None, :]
    ).astype(jnp.bfloat16)
    base_rows = tokens.astype(jnp.float32) + jnp.dot(
        venue_hot, venue_table, preferred_element_type=jnp.float32
    )
    normed = rms_norm(base_rows, attn_gain).astype(jnp.bfloat16)
    flat_qkv = w_qkv.reshape(model_width, 3 * head_dim)
    sq_index = lax.axis_index("sq")
    stream = ring_gather(normed)
    stream, w_out = lax.optimization_barrier((stream, w_out))
    rolled = jnp.dot(stream, flat_qkv, preferred_element_type=jnp.float32).astype(jnp.bfloat16)
    group_rows = rolled.shape[0]
    projected = lax.dynamic_slice_in_dim(
        jnp.concatenate([rolled, rolled], axis=0),
        (3 - sq_index) % sq_count * tok_rows,
        group_rows,
        axis=0,
    )
    queries = projected[:, :head_dim]
    keyval = projected[:, head_dim:]
    ranks = time_rank.reshape(sq_count, ex_count, tok_rows).transpose(1, 0, 2)
    ranks = ranks.reshape(ex_count, group_rows)
    core = ex_index % cores
    query_rank = lax.dynamic_index_in_dim(ranks, ex_index, 0, keepdims=False)
    near_rank = jnp.take(ranks, plane_sources(ex_index, core), axis=0, mode="clip").reshape(-1)
    far_rank = jnp.take(ranks, plane_sources(ex_index, 1 - core), axis=0, mode="clip").reshape(-1)
    near = plane_gather(keyval)
    far = core_swap(near)
    state = jnp.concatenate(
        [
            jnp.zeros((head_dim, group_rows), jnp.float32),
            jnp.full((4, group_rows), neg_large, jnp.float32),
            jnp.zeros((4, group_rows), jnp.float32),
        ],
        axis=0,
    )
    state = flash_part(queries, near, query_rank, near_rank, state)
    state = flash_part(queries, far, query_rank, far_rank, state)
    head_out = (state[:head_dim] / state[head_dim + 4 : head_dim + 5]).T.astype(jnp.bfloat16)
    regrouped = lax.all_to_all(head_out, "sq", split_axis=0, concat_axis=1, tiled=True)
    all_out = lax.all_gather(w_out, "sq", axis=0, tiled=True)
    per_head = jnp.einsum(
        "thd,hde->hte",
        regrouped.reshape(tok_rows, sq_count, head_dim),
        all_out.reshape(sq_count, head_dim, model_width),
        preferred_element_type=jnp.float32,
    ).astype(jnp.bfloat16)
    attn_sum = jnp.sum(per_head.astype(jnp.float32), axis=0)
    hidden_state = base_rows + attn_sum
    normed_ffn = rms_norm(hidden_state, ffn_gain).astype(jnp.bfloat16)
    logits = jnp.dot(normed_ffn, router, preferred_element_type=jnp.float32)
    expert_count = router.shape[1]
    top_count = routes.shape[1]
    expert_ids = jnp.arange(expert_count, dtype=jnp.int32)
    hot = jnp.any(routes[:, :, None] == expert_ids[None, None, :], axis=1)
    raw_gate = jnp.where(hot, jax.nn.sigmoid(logits), 0.0)
    gate_weights = raw_gate / jnp.sum(raw_gate, axis=1, keepdims=True)
    capacity = min(tok_rows, tok_rows * top_count * 5 // (2 * expert_count))
    capacity = -(-capacity // 16) * 16
    hot_count = hot.astype(jnp.int32)
    slot = jnp.cumsum(hot_count, axis=0) - hot_count
    slot = jnp.where(hot, slot, -1)
    taken = slot.T[:, None, :] == jnp.arange(capacity, dtype=jnp.int32)[None, :, None]
    pick = taken.astype(jnp.bfloat16).reshape(expert_count * capacity, tok_rows)
    outgoing = jnp.dot(pick, normed_ffn, preferred_element_type=jnp.float32).astype(jnp.bfloat16)
    outgoing = outgoing.reshape(expert_count, capacity, model_width)
    local_experts = expert_in.shape[0]
    arrived = lax.all_to_all(outgoing, "ex", split_axis=0, concat_axis=0, tiled=True)
    slot_count = arrived.shape[1]
    grouped = arrived.reshape(ex_count, local_experts, slot_count, model_width)
    gate_part = jnp.einsum(
        "sekd,edf->sekf", grouped, expert_in[:, 0], preferred_element_type=jnp.float32
    )
    up_part = jnp.einsum(
        "sekd,edf->sekf", grouped, expert_in[:, 1], preferred_element_type=jnp.float32
    )
    hidden = (jax.nn.silu(gate_part) * up_part).astype(jnp.bfloat16)
    produced = jnp.einsum(
        "sekf,efd->sekd", hidden, expert_out, preferred_element_type=jnp.float32
    ).astype(jnp.bfloat16)
    returned = lax.all_to_all(
        produced.reshape(ex_count * local_experts, slot_count, model_width),
        "ex",
        split_axis=0,
        concat_axis=0,
        tiled=True,
    )
    spread = jnp.where(
        slot[:, :, None] == jnp.arange(capacity, dtype=jnp.int32)[None, None, :],
        gate_weights[:, :, None],
        0.0,
    ).reshape(tok_rows, expert_count * capacity)
    coarse = spread.astype(jnp.bfloat16)
    fine = (spread - coarse.astype(jnp.float32)).astype(jnp.bfloat16)
    both = jnp.dot(
        jnp.concatenate([coarse, fine], axis=0),
        returned.reshape(expert_count * capacity, model_width),
        preferred_element_type=jnp.float32,
    )
    moe_sum = both[:tok_rows] + both[tok_rows:]
    attended = attn_sum.astype(jnp.bfloat16)
    layer_out = (hidden_state + moe_sum).astype(jnp.bfloat16)
    return (attended, layer_out)


def solution(mesh):
    placed = (
        P(("sq", "ex"), None),
        P(("sq", "ex")),
        P(),
        P(("sq", "ex"), None),
        P(),
        P(),
        P(None, None, "sq"),
        P("sq", None),
        P(),
        P(),
        P("ex", None, None, None),
        P("ex", None, None),
    )
    return jax.shard_map(
        body,
        mesh=mesh,
        in_specs=placed,
        out_specs=(P(("sq", "ex"), None), P(("sq", "ex"), None)),
        check_vma=False,
    )
```

```python
import functools
import math

import jax
import jax.numpy as jnp
from jax import lax
from jax.experimental import pallas as pl
from jax.experimental.pallas import tpu as pltpu
from jax.sharding import PartitionSpec as P

epsilon = 1e-06
neg_large = -1e30


def rms_norm(values, gain):
    mean_square = jnp.mean(values * values, axis=-1, keepdims=True)
    return values * lax.rsqrt(mean_square + epsilon) * gain


def flash_kernel(key_step, scale, query_ref, keyval_ref, query_rank_ref, key_rank_ref, state_ref, out_ref):
    head_dim = query_ref.shape[1]
    queries = query_ref[...]
    query_count = queries.shape[0]
    query_rank = query_rank_ref[...]
    out_ref[...] = state_ref[...]

    def step(j, carry):
        row_best, row_total = carry
        start = pl.multiple_of(j * key_step, key_step)
        keys = keyval_ref[pl.ds(start, key_step), :head_dim]
        values = keyval_ref[pl.ds(start, key_step), head_dim:]
        scores = lax.dot_general(
            keys, queries, (((1,), (1,)), ((), ())), preferred_element_type=jnp.float32
        )
        key_rank = key_rank_ref[pl.ds(start, key_step), :]
        key_rank = jnp.concatenate([key_rank] * (query_count // 128), axis=1)
        scores = jnp.where(key_rank <= query_rank, scores, neg_large)
        new_best = jnp.maximum(row_best, jnp.max(scores, axis=0, keepdims=True))
        probs = jnp.exp2((scores - new_best) * scale)
        factor = jnp.exp2((row_best - new_best) * scale)
        row_total = row_total * factor + jnp.sum(probs, axis=0, keepdims=True)
        update = lax.dot_general(
            values,
            probs.astype(jnp.bfloat16),
            (((0,), (0,)), ((), ())),
            preferred_element_type=jnp.float32,
        )
        out_ref[:head_dim] = out_ref[:head_dim] * factor + update
        return new_best, row_total

    carry = (state_ref[head_dim : head_dim + 1], state_ref[head_dim + 4 : head_dim + 5])
    best, total = lax.fori_loop(0, keyval_ref.shape[0] // key_step, step, carry)
    out_ref[head_dim:] = jnp.concatenate(
        [jnp.broadcast_to(best, (4, query_count)), jnp.broadcast_to(total, (4, query_count))],
        axis=0,
    )


def spread_rank(key_rank):
    return jnp.broadcast_to(key_rank[:, None], (key_rank.shape[0], 128))


def flash_part(queries, keyval, query_rank, key_rank, state):
    head_dim = queries.shape[1]
    scale = math.log2(math.e) / math.sqrt(head_dim)
    return pl.pallas_call(
        functools.partial(flash_kernel, 1024, scale),
        out_shape=jax.ShapeDtypeStruct(state.shape, jnp.float32),
        name="flash_part",
        compiler_params=pltpu.CompilerParams(vmem_limit_bytes=48 << 20),
    )(queries, keyval, query_rank[None, :], key_rank, state)


side = 4
cores = 2
hops = (0, 1, 3, 2)


def ex_id(x, y, c):
    return (x % side) * side * cores + (y % side) * cores + c


def plane_shift(array, amount, first):
    pairs = []
    for x in range(side):
        for y in range(side):
            for c in range(cores):
                if (c == 0) == first:
                    target = ex_id(x + amount, y, c)
                else:
                    target = ex_id(x, y + amount, c)
                pairs.append((ex_id(x, y, c), target))
    return lax.ppermute(array, "ex", pairs)


def plane_gather(array):
    line = jnp.concatenate(
        [array] + [plane_shift(array, s, True) for s in hops[1:]], axis=0
    )
    return jnp.concatenate([line] + [plane_shift(line, s, False) for s in hops[1:]], axis=0)


def plane_sources(ex_index, core):
    x = ex_index // (side * cores)
    y = ex_index // cores % side
    second = jnp.repeat(jnp.array(hops, jnp.int32), side)
    first = jnp.tile(jnp.array(hops, jnp.int32), side)
    shift_x = jnp.where(core == 0, first, second)
    shift_y = jnp.where(core == 0, second, first)
    return (x - shift_x) % side * side * cores + (y - shift_y) % side * cores + core


def core_swap(array):
    return lax.ppermute(array, "ex", [(i, i ^ 1) for i in range(side * side * cores)])


def ring_shift(array, amount):
    count = lax.axis_size("sq")
    return lax.ppermute(array, "sq", [(i, (i + amount) % count) for i in range(count)])


def ring_gather(array):
    half = array.shape[0] // 2
    p1 = ring_shift(array, 1)
    m1 = ring_shift(array, -1)
    p2 = ring_shift(array, 2)
    m2 = ring_shift(array, -2)
    p3 = ring_shift(p2, 1)
    m3 = ring_shift(m2, -1)
    p4 = ring_shift(p2[:half], 2)
    m4 = ring_shift(m2[half:], -2)
    return [p3, p2, p1, array, m1, m2, m3, jnp.concatenate([p4, m4], axis=0)]


def body(
    tokens,
    venue_id,
    time_rank,
    routes,
    venue_table,
    attn_gain,
    w_qkv,
    w_out,
    ffn_gain,
    router,
    expert_in,
    expert_out,
):
    tok_rows, model_width = tokens.shape
    head_dim = w_out.shape[0]
    sq_count = lax.axis_size("sq")
    ex_count = lax.axis_size("ex")
    ex_index = lax.axis_index("ex")
    venue_hot = (
        venue_id[:, None] == jnp.arange(venue_table.shape[0], dtype=jnp.int32)[None, :]
    ).astype(jnp.bfloat16)
    base_rows = tokens.astype(jnp.float32) + jnp.dot(
        venue_hot, venue_table, preferred_element_type=jnp.float32
    )
    normed = rms_norm(base_rows, attn_gain).astype(jnp.bfloat16)
    flat_qkv = w_qkv.reshape(model_width, 3 * head_dim)
    sq_index = lax.axis_index("sq")
    group_rows = sq_count * tok_rows
    ranks = time_rank.reshape(sq_count, ex_count, tok_rows).transpose(1, 0, 2)
    ranks = ranks.reshape(ex_count, group_rows)
    core = ex_index % cores
    query_rank = lax.dynamic_index_in_dim(ranks, ex_index, 0, keepdims=False)
    near_rank = jnp.take(ranks, plane_sources(ex_index, core), axis=0, mode="clip").reshape(-1)
    far_rank = jnp.take(ranks, plane_sources(ex_index, 1 - core), axis=0, mode="clip").reshape(-1)
    near_rank, far_rank = spread_rank(near_rank), spread_rank(far_rank)
    pieces = ring_gather(normed)
    late = lax.optimization_barrier((pieces[0], pieces[6], pieces[7], near_rank, far_rank))
    pieces = [late[0]] + pieces[1:6] + [late[1], late[2]]
    near_rank, far_rank = late[3:]
    projected = jnp.zeros((group_rows, 3 * head_dim), jnp.bfloat16)
    for b in (3, 2, 4, 1, 5, 0, 6, 7):
        piece = jnp.dot(pieces[b], flat_qkv, preferred_element_type=jnp.float32)
        place = (sq_index + (b + 5)) % sq_count * tok_rows
        projected = lax.dynamic_update_slice_in_dim(
            projected, piece.astype(jnp.bfloat16), place, axis=0
        )
    projected, w_out = lax.optimization_barrier((projected, w_out))
    queries = projected[:, :head_dim]
    keyval = projected[:, head_dim:]
    near = plane_gather(keyval)
    far = core_swap(near)
    state = jnp.concatenate(
        [
            jnp.zeros((head_dim, group_rows), jnp.float32),
            jnp.full((4, group_rows), neg_large, jnp.float32),
            jnp.zeros((4, group_rows), jnp.float32),
        ],
        axis=0,
    )
    state = flash_part(queries, near, query_rank, near_rank, state)
    state = flash_part(queries, far, query_rank, far_rank, state)
    head_out = (state[:head_dim] / state[head_dim + 4 : head_dim + 5]).T.astype(jnp.bfloat16)
    regrouped = lax.all_to_all(head_out, "sq", split_axis=0, concat_axis=1, tiled=True)
    all_out = lax.all_gather(w_out, "sq", axis=0, tiled=True)
    per_head = jnp.einsum(
        "thd,hde->hte",
        regrouped.reshape(tok_rows, sq_count, head_dim),
        all_out.reshape(sq_count, head_dim, model_width),
        preferred_element_type=jnp.float32,
    ).astype(jnp.bfloat16)
    attn_sum = jnp.sum(per_head.astype(jnp.float32), axis=0)
    hidden_state = base_rows + attn_sum
    normed_ffn = rms_norm(hidden_state, ffn_gain).astype(jnp.bfloat16)
    logits = jnp.dot(normed_ffn, router, preferred_element_type=jnp.float32)
    expert_count = router.shape[1]
    top_count = routes.shape[1]
    expert_ids = jnp.arange(expert_count, dtype=jnp.int32)
    hot = jnp.any(routes[:, :, None] == expert_ids[None, None, :], axis=1)
    raw_gate = jnp.where(hot, jax.nn.sigmoid(logits), 0.0)
    gate_weights = raw_gate / jnp.sum(raw_gate, axis=1, keepdims=True)
    capacity = min(tok_rows, tok_rows * top_count * 5 // (2 * expert_count))
    capacity = -(-capacity // 16) * 16
    hot_count = hot.astype(jnp.int32)
    slot = jnp.cumsum(hot_count, axis=0) - hot_count
    slot = jnp.where(hot, slot, -1)
    taken = slot.T[:, None, :] == jnp.arange(capacity, dtype=jnp.int32)[None, :, None]
    pick = taken.astype(jnp.bfloat16).reshape(expert_count * capacity, tok_rows)
    outgoing = jnp.dot(pick, normed_ffn, preferred_element_type=jnp.float32).astype(jnp.bfloat16)
    outgoing = outgoing.reshape(expert_count, capacity, model_width)
    local_experts = expert_in.shape[0]
    arrived = lax.all_to_all(outgoing, "ex", split_axis=0, concat_axis=0, tiled=True)
    slot_count = arrived.shape[1]
    grouped = arrived.reshape(ex_count, local_experts, slot_count, model_width)
    gate_part = jnp.einsum(
        "sekd,edf->sekf", grouped, expert_in[:, 0], preferred_element_type=jnp.float32
    )
    up_part = jnp.einsum(
        "sekd,edf->sekf", grouped, expert_in[:, 1], preferred_element_type=jnp.float32
    )
    hidden = (jax.nn.silu(gate_part) * up_part).astype(jnp.bfloat16)
    produced = jnp.einsum(
        "sekf,efd->sekd", hidden, expert_out, preferred_element_type=jnp.float32
    ).astype(jnp.bfloat16)
    returned = lax.all_to_all(
        produced.reshape(ex_count * local_experts, slot_count, model_width),
        "ex",
        split_axis=0,
        concat_axis=0,
        tiled=True,
    )
    spread = jnp.where(
        slot[:, :, None] == jnp.arange(capacity, dtype=jnp.int32)[None, None, :],
        gate_weights[:, :, None],
        0.0,
    ).reshape(tok_rows, expert_count * capacity)
    coarse = spread.astype(jnp.bfloat16)
    fine = (spread - coarse.astype(jnp.float32)).astype(jnp.bfloat16)
    both = jnp.dot(
        jnp.concatenate([coarse, fine], axis=0),
        returned.reshape(expert_count * capacity, model_width),
        preferred_element_type=jnp.float32,
    )
    moe_sum = both[:tok_rows] + both[tok_rows:]
    attended = attn_sum.astype(jnp.bfloat16)
    layer_out = (hidden_state + moe_sum).astype(jnp.bfloat16)
    return (attended, layer_out)


def solution(mesh):
    placed = (
        P(("sq", "ex"), None),
        P(("sq", "ex")),
        P(),
        P(("sq", "ex"), None),
        P(),
        P(),
        P(None, None, "sq"),
        P("sq", None),
        P(),
        P(),
        P("ex", None, None, None),
        P("ex", None, None),
    )
    return jax.shard_map(
        body,
        mesh=mesh,
        in_specs=placed,
        out_specs=(P(("sq", "ex"), None), P(("sq", "ex"), None)),
        check_vma=False,
    )
```
